32 devices in a mesh: grp: 2 (over x), chan: 16 (over z, y, core).
Axes of the slice: x: 2, y: 2, z: 4, core: 2. Of those that a mesh axis runs over, the one named last changes fastest.
Arguments:
- samples: bfloat16 [32, 16, 256, 1024], P(('grp', 'chan')), parts along dimension 0, may hold values from -6 to 6
- fir: float32 [16, 1024], replicated, may hold values from -1.5 to 1.5
- chan_assign: int32 [256], replicated, may hold values from 0 to 511, as said below
- input_order: int32 [1024], replicated, may hold values from 0 to 1023, each once
Outputs:
- vis: bfloat16 [512, 1024, 1024], P(('grp', 'chan')), parts along dimension 0
The draws below stay inside these ranges and needn't reach their ends.
There are 2 independent parts, one for each index of `grp`. The reference program is written for one: setup_inputs(seed, part) draws one part's arguments, and reference() takes and returns one part's arrays. A program takes and returns all parts, laid end to end along the dimension named above; an argument that names none is the same for every part. Nothing has to cross between parts.
Inputs may be any that keep to these rules, and one draw needn't show every extreme that they name: `chan_assign`: distinct transform bins; bin 0 and bin 1024 // 2 - 1 are always among them. `input_order`: each input number once.
All inputs are finite; a program needn't handle non-finite values.
Results may differ from the reference program's by a relative error of at most 0.0074.
Values may be sent and summed in bfloat16 or wider, within the bound.
No kernel may reach another device: no remote copies, remote signals or barrier semaphores. Data moves between devices by JAX's collectives and lax.ppermute only.
A program may use at most 256 MiB of HBM per device.

```python
import math
import jax
import jax.numpy as jnp
from jax import lax

INPUTS = 1024
FRAME = 1024
NCH = 256
TAPS = 16
QUART = 4
FQ = 16
SPECTRA = 64
AGROUPS = 4
IN_DEV = 256


def draw_chan_assign(key, part):
    key_middle = jax.random.fold_in(key, 11)
    key_mixing = jax.random.fold_in(key, 12)
    middle = jax.random.permutation(key_middle, FRAME // 2 - 2)[:NCH - 2].astype(jnp.int32) + 1
    ends = jnp.array([0, FRAME // 2 - 1], dtype=jnp.int32)
    values = jnp.concatenate([ends, middle])
    return jax.random.permutation(key_mixing, values).astype(jnp.int32)


def levels(rng, extent, cuts, least, high):
    gain = 1.0
    for position, parts in cuts:
        steps = jax.random.uniform(jax.random.fold_in(jax.random.fold_in(rng, 6), position), (parts,), jnp.float32, least / len(cuts), high / len(cuts))
        gain = gain * jnp.repeat(jnp.exp(steps), extent[position] // parts).reshape((-1,) + (1,) * (len(extent) - 1 - position))
    return gain


def bell_draw(own_key, extent, scale, reach, pieces=(), held_as=jnp.bfloat16):
    values = scale * jax.random.normal(own_key, extent, jnp.float32)
    if pieces:
        values = values * levels(own_key, extent, pieces, -0.22, 0.18)
    return jnp.clip(values, -reach, reach).astype(held_as)


def setup_inputs(seed: int = 0, part: int = 0) -> dict:
    keys = jax.random.split(jax.random.key(seed), 5)
    part_splits = jax.random.split(jax.random.fold_in(keys[4], part), 5)
    return {
        "samples": bell_draw(part_splits[0], (QUART * AGROUPS, FQ, IN_DEV, FRAME), 1.0, 6.0, ((0, 16),)),
        "fir": bell_draw(keys[1], (TAPS, FRAME), TAPS ** -0.5, 1.5, (), jnp.float32),
        "chan_assign": draw_chan_assign(jax.random.fold_in(keys[4], 71), part),
        "input_order": jax.random.permutation(keys[3], INPUTS).astype(jnp.int32),
    }


def make_table(chan_assign, frame_len):
    samples_index = jnp.arange(frame_len, dtype=jnp.int32)
    phase_index = chan_assign.astype(jnp.int32)[:, None] * samples_index[None, :] % frame_len
    angles = phase_index.astype(jnp.float32) * (2.0 * math.pi / frame_len)
    norm_scale = 1.0 / math.sqrt(frame_len)
    return jnp.stack([jnp.cos(angles) * norm_scale, -jnp.sin(angles) * norm_scale]).astype(jnp.bfloat16)

def reference(samples, fir, chan_assign, input_order):
    blocks = samples.reshape(QUART, AGROUPS, FQ, IN_DEV, FRAME)
    series = jnp.transpose(blocks, (0, 2, 1, 3, 4)).reshape(SPECTRA, INPUTS, FRAME)
    need = TAPS - 1
    padded = jnp.concatenate([jnp.zeros((need, INPUTS, FRAME), series.dtype), series], axis=0)
    accum = jnp.zeros((SPECTRA, INPUTS, FRAME), jnp.float32)
    for tap_index in range(TAPS):
        shifted = padded[need - tap_index:need - tap_index + SPECTRA].astype(jnp.float32)
        accum = accum + fir[tap_index][None, None, :] * shifted
    filtered = accum.astype(jnp.bfloat16)
    dft_table = make_table(chan_assign, FRAME).reshape(2 * NCH, FRAME)
    spectra = jnp.dot(filtered.reshape(SPECTRA * INPUTS, FRAME), dft_table.T, preferred_element_type=jnp.float32)
    spectra = spectra.astype(jnp.bfloat16).reshape(SPECTRA, INPUTS, 2, NCH)
    slot_of = jnp.argsort(input_order).astype(jnp.int32)
    spectra = jnp.take(spectra, slot_of, axis=1)
    per_chan = jnp.transpose(spectra, (3, 2, 0, 1))

    def correlate_one(chan_block):
        stacked = chan_block.reshape(2 * SPECTRA, INPUTS)
        auto_sum = jnp.dot(stacked.T, stacked, preferred_element_type=jnp.float32)
        cross_sum = jnp.dot(chan_block[0].T, chan_block[1], preferred_element_type=jnp.float32)
        row_index = lax.broadcasted_iota(jnp.int32, (INPUTS, INPUTS), 0)
        col_index = lax.broadcasted_iota(jnp.int32, (INPUTS, INPUTS), 1)
        packed = jnp.where(row_index <= col_index, auto_sum, cross_sum - cross_sum.T) / SPECTRA
        return packed.astype(jnp.bfloat16)
    return lax.map(correlate_one, per_chan)
```

```python
import functools
import math

import jax
import jax.numpy as jnp
from jax import lax
from jax.experimental import pallas as pl
from jax.experimental.pallas import tpu as pltpu
from jax.sharding import PartitionSpec as P

QUART = 4
LANES = 128


def make_table(chans, frame_len):
    samples_index = jnp.arange(frame_len, dtype=jnp.int32)
    phase_index = chans[:, None] * samples_index[None, :] % frame_len
    angles = phase_index.astype(jnp.float32) * (2.0 * math.pi / frame_len)
    norm_scale = 1.0 / math.sqrt(frame_len)
    table = jnp.stack([jnp.cos(angles) * norm_scale, -jnp.sin(angles) * norm_scale], axis=1)
    return table.astype(jnp.bfloat16).reshape(-1, frame_len)


def front_kernel(sets, x_ref, fir_ref, table_ref, *rest):
    outs, (filt, spread) = rest[: 2 * sets], rest[2 * sets :]
    frames, slots, lanes = x_ref.shape
    taps = fir_ref.shape[0]
    step = pl.program_id(0)
    columns = pl.ds(pl.multiple_of(step * lanes, lanes), lanes)

    def filter_rows(block, carry):
        rows = pl.ds(pl.multiple_of(block * 16, 16), 16)
        own = [x_ref[f, rows, :].astype(jnp.float32) for f in range(frames)]
        for out in range(2 * frames):
            total = None
            for source in range(max(0, out - taps + 1), min(frames, out + 1)):
                term = own[source] * fir_ref[out - source : out - source + 1, :]
                total = term if total is None else total + term
            if total is None:
                total = jnp.zeros((16, lanes), jnp.float32)
            filt[out, rows, columns] = total.astype(jnp.bfloat16)
        return carry

    lax.fori_loop(0, slots // 16, filter_rows, 0)

    @pl.when(step == pl.num_programs(0) - 1)
    def _():
        table_rows = table_ref.shape[0] // sets
        pair = 2 if slots % LANES == 0 else 1
        for part in range(2):
            for each in range(sets):
                table = table_ref[each * table_rows : (each + 1) * table_rows, :]

                def transform(index, carry):
                    frame = index * pair
                    block = filt[pl.ds(part * frames + frame, pair)]
                    result = lax.dot_general(
                        table,
                        block.reshape(pair * slots, -1),
                        (((1,), (1,)), ((), ())),
                        preferred_element_type=jnp.float32,
                    )
                    for one in range(pair):
                        spread[pl.ds(frame + one, table_rows, stride=frames), :] = result[
                            :, one * slots : (one + 1) * slots
                        ]
                    return carry

                lax.fori_loop(0, frames // pair, transform, 0)
                outs[part * sets + each][...] = spread[...].astype(jnp.bfloat16)


def front(x, fir, table, block, blocks, sets):
    frames, slots_dev, frame_len = x.shape
    slots = slots_dev // blocks
    table_rows = table.shape[0]
    out_rows = table_rows // sets * frames
    return pl.pallas_call(
        functools.partial(front_kernel, sets),
        grid=(frame_len // LANES,),
        in_specs=[
            pl.BlockSpec((frames, slots, LANES), lambda j: (0, block, j)),
            pl.BlockSpec((fir.shape[0], LANES), lambda j: (0, j)),
            pl.BlockSpec((table_rows, frame_len), lambda j: (0, 0), pipeline_mode=pl.Buffered(1)),
        ],
        out_specs=[pl.BlockSpec((out_rows, slots), lambda j: (0, 0), pipeline_mode=pl.Buffered(1))]
        * (2 * sets),
        out_shape=[jax.ShapeDtypeStruct((out_rows, slots), jnp.bfloat16)] * (2 * sets),
        scratch_shapes=[
            pltpu.VMEM((2 * frames, slots, frame_len), jnp.bfloat16),
            pltpu.VMEM((out_rows, slots), jnp.float32),
        ],
        cost_estimate=pl.CostEstimate(
            flops=4 * frames * slots * frame_len * table_rows,
            bytes_accessed=2 * frames * slots * frame_len + 4 * table_rows * frames * slots,
            transcendentals=0,
        ),
        name="front",
    )(x, fir, table)


def back_kernel(blocks, groups, scale, *refs):
    order_ref, datas = refs[0], refs[1 : 1 + blocks]
    out_ref, pick, ordered = refs[-3], refs[-2], refs[-1]
    inputs = out_ref.shape[-1]
    tile = min(256, inputs)

    @pl.when(pl.program_id(0) == 0)
    def _():
        for first in range(0, inputs, tile):
            wanted = first + lax.broadcasted_iota(jnp.int32, (tile, inputs), 0)
            hit = jnp.where(order_ref[...] == wanted, 1.0, 0.0)
            pick[first : first + tile, :] = hit.astype(jnp.bfloat16)

    pieces = []
    for group in range(groups):
        for data in datas:
            planes = data.shape[1] // 2
            real, imag = [], []
            for quarter in range(QUART):
                source = quarter * groups + group
                real.append(data[source, :planes, :])
                imag.append(data[source, planes:, :])
            rows = []
            for quarter in range(QUART):
                rows += [real[quarter], imag[quarter]]
            for quarter in range(QUART):
                rows += [imag[quarter], -real[quarter]]
            pieces.append(jnp.concatenate(rows, axis=0))
    stacked = jnp.concatenate(pieces, axis=1)
    depth = stacked.shape[0] // 2
    contract = (((1,), (1,)), ((), ()))
    for first in range(0, inputs, tile):
        part = pl.ds(first, tile)
        ordered[part, :] = lax.dot_general(
            pick[part, :], stacked, contract, preferred_element_type=jnp.float32
        ).astype(jnp.bfloat16)
    for first in range(0, inputs, tile):
        left = ordered[first : first + tile, :depth]
        for other in range(0, inputs, tile):
            place = pl.ds(other, tile)
            if other >= first:
                upper = lax.dot_general(
                    left, ordered[place, :depth], contract, preferred_element_type=jnp.float32
                )
            if other <= first:
                lower = lax.dot_general(
                    left, ordered[place, depth:], contract, preferred_element_type=jnp.float32
                )
            if other > first:
                result = upper
            elif other < first:
                result = lower
            else:
                row = lax.broadcasted_iota(jnp.int32, (tile, tile), 0)
                column = lax.broadcasted_iota(jnp.int32, (tile, tile), 1)
                result = jnp.where(row <= column, upper, lower)
            out_ref[0, first : first + tile, place] = (result * scale).astype(jnp.bfloat16)


def back(order, datas, each, sets, chan_dev, earlier):
    sources, rows, slots = datas[0].shape
    inputs = order.shape[1]
    groups = sources // QUART
    held = chan_dev // sets
    per_chan = rows // held
    spectra_total = QUART * (per_chan // 2)
    operands = [order] + list(datas)
    in_specs = [pl.BlockSpec((1, inputs), lambda k: (0, 0))]
    in_specs += [pl.BlockSpec((sources, per_chan, slots), lambda k: (0, k, 0))] * len(datas)
    aliases = {}
    kernel = functools.partial(back_kernel, len(datas), groups, 1.0 / spectra_total)
    if earlier is not None:
        aliases = {len(operands): 0}
        operands.append(earlier)
        in_specs.append(pl.BlockSpec(memory_space=pl.ANY))
    return pl.pallas_call(
        kernel,
        grid=(held,),
        in_specs=in_specs,
        out_specs=pl.BlockSpec((1, inputs, inputs), lambda k: (k + each * held, 0, 0)),
        out_shape=jax.ShapeDtypeStruct((chan_dev, inputs, inputs), jnp.bfloat16),
        scratch_shapes=[
            pltpu.VMEM((inputs, inputs), jnp.bfloat16),
            pltpu.VMEM((inputs, 4 * QUART * (per_chan // 2)), jnp.bfloat16),
        ],
        input_output_aliases=aliases,
        cost_estimate=pl.CostEstimate(
            flops=held * inputs * inputs * 1024,
            bytes_accessed=2 * held * inputs * inputs,
            transcendentals=0,
        ),
        name="back",
    )(*operands)


def on_device(samples, fir, chan_assign, input_order):
    own_frames = samples[0]
    frames, slots_dev, frame_len = own_frames.shape
    chan_count = lax.axis_size("chan")
    group_count = chan_count // QUART
    chan_dev = chan_assign.shape[0] // chan_count
    sets = 2 if chan_dev % 2 == 0 else 1
    held = chan_dev // sets
    blocks = 2 if slots_dev % (2 * LANES) == 0 else 1
    chans = chan_assign.reshape(chan_count, sets, held).transpose(1, 0, 2).reshape(-1)
    table = make_table(chans, frame_len)
    order = input_order[None, :]
    per_dest = held * 2 * frames

    ready = [[None] * blocks for _ in range(sets)]
    for block in range(blocks):
        parts = front(own_frames, fir, table, block, blocks, sets)
        for each in range(sets):
            both = jnp.concatenate(
                [
                    parts[part * sets + each].reshape(chan_count, per_dest, -1)
                    for part in range(2)
                ],
                axis=1,
            )
            got = lax.all_to_all(both, "chan", split_axis=0, concat_axis=0, tiled=True)
            own = got[:, :per_dest].astype(jnp.float32)
            late = got[: chan_count - group_count, per_dest:].astype(jnp.float32)
            late = jnp.pad(late, ((group_count, 0), (0, 0), (0, 0)))
            ready[each][block] = (own + late).astype(jnp.bfloat16)
    vis = None
    for each in range(sets):
        vis = back(order, ready[each], each, sets, chan_dev, vis)
    return vis


def solution(mesh):
    in_specs = (P(("grp", "chan"), None, None, None), P(), P(), P())
    out_specs = P(("grp", "chan"), None, None)
    return jax.shard_map(
        on_device, mesh=mesh, in_specs=in_specs, out_specs=out_specs, check_vma=False
    )
```

```python
import functools
import math

import jax
import jax.numpy as jnp
from jax import lax
from jax.experimental import pallas as pl
from jax.experimental.pallas import tpu as pltpu
from jax.sharding import PartitionSpec as P

QUART = 4
LANES = 128


def split_table(chans, frame_len):
    norm_scale = 1.0 / math.sqrt(frame_len)

    def angles(samples):
        phase_index = chans[:, None] * samples[None, :] % frame_len
        return phase_index.astype(jnp.float32) * (2.0 * math.pi / frame_len)

    fine = angles(jnp.arange(LANES, dtype=jnp.int32))
    coarse = angles(jnp.arange(0, frame_len, LANES, dtype=jnp.int32)).T[:, :, None]
    fine = jnp.stack([jnp.cos(fine) * norm_scale, jnp.sin(fine) * norm_scale])
    return fine, jnp.stack([jnp.cos(coarse), jnp.sin(coarse)], axis=1)


def tap_leaves(taps):
    if len(taps) <= 4:
        return [taps]
    low, high = taps[: len(taps) // 2], taps[len(taps) // 2 :]
    middle = [one + other for one, other in zip(low, high)]
    return tap_leaves(low) + tap_leaves(high) + tap_leaves(middle)


def direct(values, taps):
    outs = []
    for out in range(len(values) + len(taps) - 1):
        total = None
        for source in range(max(0, out - len(taps) + 1), min(len(values), out + 1)):
            term = values[source] * taps[out - source]
            total = term if total is None else total + term
        outs.append(total)
    return outs


def product(values, leaves):
    count = len(values)
    if count <= 4:
        return direct(values, next(leaves))
    half = count // 2
    low = product(values[:half], leaves)
    high = product(values[half:], leaves)
    middle = product([one + other for one, other in zip(values[:half], values[half:])], leaves)
    middle = [whole - (one + other) for whole, one, other in zip(middle, low, high)]
    outs = low[:half]
    outs += [low[half + i] + middle[i] for i in range(half - 1)]
    outs += [middle[half - 1]]
    outs += [middle[half + i] + high[i] for i in range(half - 1)]
    return outs + high[half - 1 :]


def front_kernel(sets, x_ref, fir_ref, fine_ref, coarse_ref, *rest):
    outs, (filt, spread, table, coeffs) = rest[:sets], rest[sets:]
    frames, slots, lanes = x_ref.shape
    taps = fir_ref.shape[0]
    step = pl.program_id(0)
    columns = pl.ds(pl.multiple_of(step * lanes, lanes), lanes)
    recursive = taps == frames and frames & (frames - 1) == 0

    chans = fine_ref.shape[1]
    turn = [coarse_ref[0, part] for part in range(2)]
    held = chans // sets
    rows = [fine_ref[0] * turn[0] - fine_ref[1] * turn[1]]
    rows += [-(fine_ref[1] * turn[0] + fine_ref[0] * turn[1])]
    for each in range(sets):
        for part in range(2):
            first = (each * 2 + part) * held
            piece = rows[part][each * held : (each + 1) * held]
            table[first : first + held, columns] = piece.astype(jnp.bfloat16)

    leaves = [fir_ref[tap : tap + 1, :] for tap in range(taps)]
    leaves = tap_leaves(leaves) if recursive else [leaves]
    sizes = [len(leaf) for leaf in leaves]
    for index, row in enumerate(sum(leaves, [])):
        coeffs[index : index + 1, :] = row

    def filter_rows(block, carry):
        rows = pl.ds(pl.multiple_of(block * 16, 16), 16)
        own = [x_ref[f, rows, :].astype(jnp.float32) for f in range(frames)]
        done = []
        for half in range(2):
            values = [one[half * 8 : half * 8 + 8] for one in own]
            starts = [sum(sizes[:i]) for i in range(len(sizes))]
            lists = [
                [coeffs[start + i : start + i + 1, :] for i in range(size)]
                for start, size in zip(starts, sizes)
            ]
            results = product(values, iter(lists)) if recursive else direct(values, lists[0])
            done.append(results)
        for out in range(2 * frames):
            if out < len(done[0]):
                total = jnp.concatenate([done[0][out], done[1][out]], axis=0)
            else:
                total = jnp.zeros((16, lanes), jnp.float32)
            filt[out, rows, columns] = total.astype(jnp.bfloat16)
        return carry

    lax.fori_loop(0, slots // 16, filter_rows, 0)

    @pl.when(step == pl.num_programs(0) - 1)
    def _():
        pair = 2 if slots % LANES == 0 else 1
        for part in range(2):

            def transform(index, carry):
                frame = index * pair
                block = filt[pl.ds(part * frames + frame, pair)]
                result = lax.dot_general(
                    table[...],
                    block.reshape(pair * slots, -1),
                    (((1,), (1,)), ((), ())),
                    preferred_element_type=jnp.float32,
                )
                for one in range(pair):
                    for piece in range(2 * sets):
                        each, which = divmod(piece, 2)
                        start = each * held * 2 * frames + which * frames
                        spread[pl.ds(start + frame + one, held, stride=2 * frames), :] = result[
                            piece * held : (piece + 1) * held, one * slots : (one + 1) * slots
                        ]
                return carry

            lax.fori_loop(0, frames // pair, transform, 0)
            for each in range(sets):
                dests, both_rows, _ = outs[each].shape
                per_dest = both_rows // 2
                block = spread[each * dests * per_dest : (each + 1) * dests * per_dest, :]
                outs[each][:, part * per_dest : (part + 1) * per_dest, :] = block.reshape(
                    dests, per_dest, slots
                ).astype(jnp.bfloat16)


def front(x, fir, fine, coarse, block, blocks, sets, dests):
    frames, slots_dev, frame_len = x.shape
    slots = slots_dev // blocks
    taps = fir.shape[0]
    chans = fine.shape[1]
    out_shape = (dests, chans // sets // dests * 4 * frames, slots)
    return pl.pallas_call(
        functools.partial(front_kernel, sets),
        grid=(frame_len // LANES,),
        in_specs=[
            pl.BlockSpec((frames, slots, LANES), lambda j: (0, block, j)),
            pl.BlockSpec((taps, LANES), lambda j: (0, j)),
            pl.BlockSpec(fine.shape, lambda j: (0, 0, 0), pipeline_mode=pl.Buffered(1)),
            pl.BlockSpec((1, 2, chans, 1), lambda j: (j, 0, 0, 0)),
        ],
        out_specs=[pl.BlockSpec(out_shape, lambda j: (0, 0, 0), pipeline_mode=pl.Buffered(1))]
        * sets,
        out_shape=[jax.ShapeDtypeStruct(out_shape, jnp.bfloat16)] * sets,
        scratch_shapes=[
            pltpu.VMEM((2 * frames, slots, frame_len), jnp.bfloat16),
            pltpu.VMEM((2 * chans * frames, slots), jnp.float32),
            pltpu.VMEM((2 * chans, frame_len), jnp.bfloat16),
            pltpu.VMEM((4 * taps, LANES), jnp.float32),
        ],
        cost_estimate=pl.CostEstimate(
            flops=8 * frames * slots * frame_len * chans,
            bytes_accessed=2 * frames * slots * frame_len + 8 * chans * frames * slots,
            transcendentals=0,
        ),
        name="front",
    )(x, fir, fine, coarse)


def back_kernel(blocks, groups, pair, scale, *refs):
    order_ref, owns, lates = refs[0], refs[1 : 1 + blocks], refs[1 + blocks : 1 + 2 * blocks]
    out_ref, pick, ordered, turned = refs[-4:]
    inputs = out_ref.shape[-1]
    tile = min(256, inputs)

    @pl.when(pl.program_id(0) == 0)
    def _():
        for first in range(0, inputs, tile):
            wanted = first + lax.broadcasted_iota(jnp.int32, (tile, inputs), 0)
            hit = jnp.where(order_ref[...] == wanted, 1.0, 0.0)
            pick[first : first + tile, :] = hit.astype(jnp.bfloat16)

    per_chan = owns[0].shape[1] // pair
    frames = per_chan // 2
    pieces = []
    for group in range(groups):
        for own, late in zip(owns, lates):
            rows = []
            for chan in range(pair):
                for part in range(2):
                    here = slice((2 * chan + part) * frames, (2 * chan + part + 1) * frames)
                    rows.append(own[group, here, :])
                    for quarter in range(1, QUART):
                        total = own[quarter * groups + group, here, :].astype(jnp.float32)
                        before = late[(quarter - 1) * groups + group, here, :]
                        rows.append((total + before.astype(jnp.float32)).astype(jnp.bfloat16))
            pieces.append(jnp.concatenate(rows, axis=0))
    stacked = jnp.concatenate(pieces, axis=1)
    depth = stacked.shape[0] // pair
    contract = (((1,), (1,)), ((), ()))
    lane = lax.broadcasted_iota(jnp.int32, (tile, depth), 1)
    sign = jnp.where(lane < depth // 2, 1.0, -1.0)
    for first in range(0, inputs, tile):
        part = pl.ds(first, tile)
        result = lax.dot_general(
            pick[part, :], stacked, contract, preferred_element_type=jnp.float32
        )
        ordered[part, :] = result.astype(jnp.bfloat16)
        for chan in range(pair):
            lanes = slice(chan * depth, (chan + 1) * depth)
            swapped = pltpu.roll(result[:, lanes], depth // 2, 1) * sign
            turned[part, lanes] = swapped.astype(jnp.bfloat16)
    for chan in range(pair):
        lanes = slice(chan * depth, (chan + 1) * depth)
        for first in range(0, inputs, tile):
            left = ordered[first : first + tile, lanes]
            for other in range(0, inputs, tile):
                place = pl.ds(other, tile)
                if other >= first:
                    upper = lax.dot_general(
                        left, ordered[place, lanes], contract, preferred_element_type=jnp.float32
                    )
                if other <= first:
                    lower = lax.dot_general(
                        left, turned[place, lanes], contract, preferred_element_type=jnp.float32
                    )
                if other > first:
                    result = upper
                elif other < first:
                    result = lower
                else:
                    row = lax.broadcasted_iota(jnp.int32, (tile, tile), 0)
                    column = lax.broadcasted_iota(jnp.int32, (tile, tile), 1)
                    result = jnp.where(row <= column, upper, lower)
                out_ref[chan, first : first + tile, place] = (result * scale).astype(jnp.bfloat16)


def back(order, datas, each, sets, chan_dev, earlier):
    sources, both_rows, slots = datas[0].shape
    inputs = order.shape[1]
    groups = sources // QUART
    held = chan_dev // sets
    pair = 2 if held % 2 == 0 else 1
    steps = held // pair
    block_rows = both_rows // 2 // steps
    depth = QUART * block_rows // pair
    block_shape = (sources, block_rows, slots)
    operands = [order] + list(datas) + list(datas)
    in_specs = [pl.BlockSpec((1, inputs), lambda k: (0, 0))]
    in_specs += [pl.BlockSpec(block_shape, lambda k: (0, k, 0))] * len(datas)
    in_specs += [pl.BlockSpec(block_shape, lambda k: (0, steps + k, 0))] * len(datas)
    aliases = {}
    scale = 1.0 / (QUART * block_rows // (2 * pair))
    if earlier is not None:
        aliases = {len(operands): 0}
        operands.append(earlier)
        in_specs.append(pl.BlockSpec(memory_space=pl.ANY))
    return pl.pallas_call(
        functools.partial(back_kernel, len(datas), groups, pair, scale),
        grid=(steps,),
        in_specs=in_specs,
        out_specs=pl.BlockSpec((pair, inputs, inputs), lambda k: (k + each * steps, 0, 0)),
        out_shape=jax.ShapeDtypeStruct((chan_dev, inputs, inputs), jnp.bfloat16),
        scratch_shapes=[
            pltpu.VMEM((inputs, inputs), jnp.bfloat16),
            pltpu.VMEM((inputs, pair * depth), jnp.bfloat16),
            pltpu.VMEM((inputs, pair * depth), jnp.bfloat16),
        ],
        input_output_aliases=aliases,
        cost_estimate=pl.CostEstimate(
            flops=held * inputs * inputs * 1024,
            bytes_accessed=2 * held * inputs * inputs,
            transcendentals=0,
        ),
        name="back",
    )(*operands)


def on_device(samples, fir, chan_assign, input_order):
    own_frames = samples[0]
    frames, slots_dev, frame_len = own_frames.shape
    chan_count = lax.axis_size("chan")
    chan_dev = chan_assign.shape[0] // chan_count
    sets = 2 if chan_dev % 2 == 0 else 1
    held = chan_dev // sets
    blocks = 2 if slots_dev % (2 * LANES) == 0 else 1
    chans = chan_assign.reshape(chan_count, sets, held).transpose(1, 0, 2).reshape(-1)
    fine, coarse = split_table(chans, frame_len)
    order = input_order[None, :]

    ready = [[None] * blocks for _ in range(sets)]
    for block in range(blocks):
        parts = front(own_frames, fir, fine, coarse, block, blocks, sets, chan_count)
        for each in range(sets):
            ready[each][block] = lax.all_to_all(
                parts[each], "chan", split_axis=0, concat_axis=0, tiled=True
            )
    vis = None
    for each in range(sets):
        vis = back(order, ready[each], each, sets, chan_dev, vis)
    return vis


def solution(mesh):
    in_specs = (P(("grp", "chan"), None, None, None), P(), P(), P())
    out_specs = P(("grp", "chan"), None, None)
    return jax.shard_map(
        on_device, mesh=mesh, in_specs=in_specs, out_specs=out_specs, check_vma=False
    )
```

```python
import functools
import math

import jax
import jax.numpy as jnp
from jax import lax
from jax.experimental import pallas as pl
from jax.experimental.pallas import tpu as pltpu
from jax.sharding import PartitionSpec as P


QUART = 4
LANES = 128


def split_table(chans, frame_len):
    norm_scale = 1.0 / math.sqrt(frame_len)

    def angles(samples):
        phase_index = chans[:, None] * samples[None, :] % frame_len
        return phase_index.astype(jnp.float32) * (2.0 * math.pi / frame_len)

    fine = angles(jnp.arange(LANES, dtype=jnp.int32))
    coarse = angles(jnp.arange(0, frame_len, LANES, dtype=jnp.int32)).T[:, :, None]
    fine = jnp.stack([jnp.cos(fine) * norm_scale, jnp.sin(fine) * norm_scale])
    return fine, jnp.stack([jnp.cos(coarse), jnp.sin(coarse)], axis=1)


def tap_leaves(taps):
    if len(taps) <= 4:
        return [taps]
    low, high = taps[: len(taps) // 2], taps[len(taps) // 2 :]
    middle = [one + other for one, other in zip(low, high)]
    return tap_leaves(low) + tap_leaves(high) + tap_leaves(middle)


def direct(values, taps):
    outs = []
    for out in range(len(values) + len(taps) - 1):
        total = None
        for source in range(max(0, out - len(taps) + 1), min(len(values), out + 1)):
            term = values[source] * taps[out - source]
            total = term if total is None else total + term
        outs.append(total)
    return outs


def product(values, leaves):
    count = len(values)
    if count <= 4:
        return direct(values, next(leaves))
    half = count // 2
    low = product(values[:half], leaves)
    high = product(values[half:], leaves)
    middle = product([one + other for one, other in zip(values[:half], values[half:])], leaves)
    middle = [whole - (one + other) for whole, one, other in zip(middle, low, high)]
    outs = low[:half]
    outs += [low[half + i] + middle[i] for i in range(half - 1)]
    outs += [middle[half - 1]]
    outs += [middle[half + i] + high[i] for i in range(half - 1)]
    return outs + high[half - 1 :]


def front_kernel(groups, x_ref, fir_ref, fine_ref, coarse_ref, *rest):
    outs, (filt, table, coeffs, spread) = rest[:-4], rest[-4:]
    sets = sum(len(members) for members, _ in groups)
    frames, slots, lanes = x_ref.shape
    taps = fir_ref.shape[0]
    step = pl.program_id(0)
    columns = pl.ds(pl.multiple_of(step * lanes, lanes), lanes)
    recursive = taps == frames and frames & (frames - 1) == 0

    chans = fine_ref.shape[1]
    turn = [coarse_ref[0, part] for part in range(2)]
    held = chans // sets
    rows = [fine_ref[0] * turn[0] - fine_ref[1] * turn[1]]
    rows += [-(fine_ref[1] * turn[0] + fine_ref[0] * turn[1])]
    for each in range(sets):
        for part in range(2):
            first = (each * 2 + part) * held
            piece = rows[part][each * held : (each + 1) * held]
            table[first : first + held, columns] = piece.astype(jnp.bfloat16)

    leaves = [fir_ref[tap : tap + 1, :] for tap in range(taps)]
    leaves = tap_leaves(leaves) if recursive else [leaves]
    sizes = [len(leaf) for leaf in leaves]
    for index, row in enumerate(sum(leaves, [])):
        coeffs[index : index + 1, :] = row

    def filter_rows(block, carry):
        rows = pl.ds(pl.multiple_of(block * 16, 16), 16)
        own = [x_ref[f, rows, :].astype(jnp.float32) for f in range(frames)]
        done = []
        for half in range(2):
            values = [one[half * 8 : half * 8 + 8] for one in own]
            starts = [sum(sizes[:i]) for i in range(len(sizes))]
            lists = [
                [coeffs[start + i : start + i + 1, :] for i in range(size)]
                for start, size in zip(starts, sizes)
            ]
            results = product(values, iter(lists)) if recursive else direct(values, lists[0])
            done.append(results)
        for out in range(2 * frames):
            if out < len(done[0]):
                total = jnp.concatenate([done[0][out], done[1][out]], axis=0)
            else:
                total = jnp.zeros((16, lanes), jnp.float32)
            filt[out, rows, columns] = total.astype(jnp.bfloat16)
        return carry

    lax.fori_loop(0, slots // 16, filter_rows, 0)

    def deliver(part, each, which, values):
        first = 0
        for members, whole in groups:
            refs = outs[first : first + (1 if whole else 2 * QUART)]
            first += len(refs)
            if each not in members:
                continue
            if whole:
                dests, _, per_dest = refs[0].shape[:3]
                refs[0][:, part, :, which] = values.reshape(dests, per_dest, frames, slots)
            else:
                _, plane, per_dest = refs[0].shape[:3]
                values = values.reshape(QUART, plane, per_dest, frames, slots)
                for target in range(QUART):
                    out = refs[part * QUART + target]
                    out[members.index(each), :, :, which] = values[target]

    @pl.when(step == pl.num_programs(0) - 1)
    def _():
        contract = (((1,), (1,)), ((), ()))
        for part in range(2):
            if slots % LANES == 0:
                result = lax.dot_general(
                    table[...],
                    filt[part * frames : (part + 1) * frames].reshape(frames * slots, -1),
                    contract,
                    preferred_element_type=jnp.float32,
                )
                result = result.reshape(-1, frames, slots)
                for piece in range(2 * sets):
                    values = result[piece * held : (piece + 1) * held].astype(jnp.bfloat16)
                    deliver(part, piece // 2, piece % 2, values)
            else:

                def transform(frame, carry):
                    result = lax.dot_general(
                        table[...],
                        filt[part * frames + frame],
                        contract,
                        preferred_element_type=jnp.float32,
                    )
                    spread[pl.ds(frame, 2 * chans, stride=frames), :] = result
                    return carry

                lax.fori_loop(0, frames, transform, 0)
                for piece in range(2 * sets):
                    values = spread[piece * held * frames : (piece + 1) * held * frames, :]
                    values = values.astype(jnp.bfloat16).reshape(held, frames, slots)
                    deliver(part, piece // 2, piece % 2, values)


def front(x, fir, fine, coarse, block, blocks, groups, dests):
    frames, slots_dev, frame_len = x.shape
    slots = slots_dev // blocks
    taps = fir.shape[0]
    chans = fine.shape[1]
    sets = sum(len(members) for members, _ in groups)
    tail = (chans // sets // dests, 2, frames, slots)
    shapes = []
    for members, whole in groups:
        if whole:
            shapes += [(dests, 2, tail[0], *tail[1:])]
        else:
            shapes += [(len(members), dests // QUART, *tail)] * (2 * QUART)
    spread = (8, LANES) if slots % LANES == 0 else (2 * chans * frames, slots)
    return pl.pallas_call(
        functools.partial(front_kernel, groups),
        grid=(frame_len // LANES,),
        in_specs=[
            pl.BlockSpec((frames, slots, LANES), lambda j: (0, block, j)),
            pl.BlockSpec((taps, LANES), lambda j: (0, j)),
            pl.BlockSpec(fine.shape, lambda j: (0, 0, 0), pipeline_mode=pl.Buffered(1)),
            pl.BlockSpec((1, 2, chans, 1), lambda j: (j, 0, 0, 0)),
        ],
        out_specs=[
            pl.BlockSpec(shape, lambda j: (0, 0, 0, 0, 0, 0), pipeline_mode=pl.Buffered(1))
            for shape in shapes
        ],
        out_shape=[jax.ShapeDtypeStruct(shape, jnp.bfloat16) for shape in shapes],
        scratch_shapes=[
            pltpu.VMEM((2 * frames, slots, frame_len), jnp.bfloat16),
            pltpu.VMEM((2 * chans, frame_len), jnp.bfloat16),
            pltpu.VMEM((4 * taps, LANES), jnp.float32),
            pltpu.VMEM(spread, jnp.float32),
        ],
        cost_estimate=pl.CostEstimate(
            flops=8 * frames * slots * frame_len * chans,
            bytes_accessed=2 * frames * slots * frame_len + 8 * chans * frames * slots,
            transcendentals=0,
        ),
        name="front",
    )(x, fir, fine, coarse)


def meet_kernel(sets, where_ref, *refs):
    owns, lates = refs[:QUART], refs[QUART : 2 * QUART]
    risen, fallen = refs[2 * QUART : 3 * QUART - 1], refs[3 * QUART - 1 : 4 * QUART - 2]
    outs, side = refs[4 * QUART - 2 : -1], refs[-1]
    here = where_ref[0]

    def add(one, other):
        return (one.astype(jnp.float32) + other.astype(jnp.float32)).astype(jnp.bfloat16)

    for target in range(QUART):

        @pl.when(here <= target)
        def _():
            for each in range(sets):
                own = owns[target][each, 0]
                outs[each][target, 0] = add(own, risen[target - 1][each, 0]) if target else own

        if target == QUART - 1:
            continue

        @pl.when(here > target)
        def _():
            for each in range(sets):
                outs[each][target, 0] = add(fallen[target][each, 0], lates[target][each, 0])

        @pl.when(here == target)
        def _():
            for each in range(sets):
                side[0, each] = add(fallen[target][each, 0], lates[target][each, 0])

    @pl.when(here == QUART - 1)
    def _():
        side[...] = jnp.zeros_like(side)


def meet(quarter, owns, lates, risen, fallen):
    sets, plane, *tail = owns[0].shape
    block = pl.BlockSpec((sets, 1, *tail), lambda g, _: (0, g, 0, 0, 0, 0))
    out = pl.BlockSpec((QUART, 1, *tail), lambda g, _: (0, g, 0, 0, 0, 0))
    side = pl.BlockSpec((1, sets, *tail), lambda g, _: (g, 0, 0, 0, 0, 0))
    shapes = [(QUART, plane, *tail)] * sets + [(plane, sets, *tail)]
    operands = [*owns, *lates, *risen, *fallen]
    return pl.pallas_call(
        functools.partial(meet_kernel, sets),
        grid_spec=pltpu.PrefetchScalarGridSpec(
            num_scalar_prefetch=1,
            grid=(plane,),
            in_specs=[block] * len(operands),
            out_specs=[out] * sets + [side],
        ),
        out_shape=[jax.ShapeDtypeStruct(shape, jnp.bfloat16) for shape in shapes],
        cost_estimate=pl.CostEstimate(
            flops=sets * owns[0].size * 5, bytes_accessed=owns[0].size * 40, transcendentals=0
        ),
        name="meet",
    )(quarter, *operands)


def back_kernel(kinds, groups, pair, scale, where_ref, order_ref, *refs):
    firsts, seconds = refs[: len(kinds)], refs[len(kinds) : 2 * len(kinds)]
    out_ref, pick, ordered, turned = refs[-4:]
    inputs = out_ref.shape[-1]
    tile = min(256, inputs)
    here = where_ref[0]

    @pl.when(pl.program_id(0) == 0)
    def _():
        for first in range(0, inputs, tile):
            wanted = first + lax.broadcasted_iota(jnp.int32, (tile, inputs), 0)
            hit = jnp.where(order_ref[...] == wanted, 1.0, 0.0)
            pick[first : first + tile, :] = hit.astype(jnp.bfloat16)

    def rows_of(kind, first, second, group, place, chan, part):
        if kind == "whole":
            if place == 0:
                return first[group, 0, chan, part]
            quarter = jnp.where(place <= here, place, place + 1)
            if place == QUART - 1:
                quarter = jnp.minimum(here + 1, QUART - 1)
            own = first[quarter * groups + group, 0, chan, part].astype(jnp.float32)
            before = second[(quarter - 1) * groups + group, 0, chan, part].astype(jnp.float32)
            return (own + before).astype(jnp.bfloat16)
        value = first[place * groups + group, chan, part]
        if place == QUART - 1:
            value = jnp.where(here < QUART - 1, second[group, 0, chan, part], value)
        return value

    pieces = []
    for group in range(groups):
        for kind, first, second in zip(kinds, firsts, seconds):
            rows = []
            for chan in range(pair):
                for part in range(2):
                    for place in range(QUART):
                        rows.append(rows_of(kind, first, second, group, place, chan, part))
            pieces.append(jnp.concatenate(rows, axis=0))
    stacked = jnp.concatenate(pieces, axis=1)
    depth = stacked.shape[0] // pair
    contract = (((1,), (1,)), ((), ()))
    lane = lax.broadcasted_iota(jnp.int32, (tile, depth), 1)
    sign = jnp.where(lane < depth // 2, 1.0, -1.0)
    for first in range(0, inputs, tile):
        part = pl.ds(first, tile)
        result = lax.dot_general(
            pick[part, :], stacked, contract, preferred_element_type=jnp.float32
        )
        ordered[part, :] = result.astype(jnp.bfloat16)
        for chan in range(pair):
            lanes = slice(chan * depth, (chan + 1) * depth)
            swapped = pltpu.roll(result[:, lanes], depth // 2, 1) * sign
            turned[part, lanes] = swapped.astype(jnp.bfloat16)
    for chan in range(pair):
        lanes = slice(chan * depth, (chan + 1) * depth)
        for first in range(0, inputs, tile):
            left = ordered[first : first + tile, lanes]
            for other in range(0, inputs, tile):
                place = pl.ds(other, tile)
                if other >= first:
                    upper = lax.dot_general(
                        left, ordered[place, lanes], contract, preferred_element_type=jnp.float32
                    )
                if other <= first:
                    lower = lax.dot_general(
                        left, turned[place, lanes], contract, preferred_element_type=jnp.float32
                    )
                if other > first:
                    result = upper
                elif other < first:
                    result = lower
                else:
                    row = lax.broadcasted_iota(jnp.int32, (tile, tile), 0)
                    column = lax.broadcasted_iota(jnp.int32, (tile, tile), 1)
                    result = jnp.where(row <= column, upper, lower)
                out_ref[chan, first : first + tile, place] = (result * scale).astype(jnp.bfloat16)


def back(quarter, order, datas, each, sets, chan_dev, earlier):
    inputs = order.shape[1]
    held = chan_dev // sets
    pair = 2 if held % 2 == 0 else 1
    steps = held // pair
    sources, (frames, slots) = datas[0][1].shape[0], datas[0][1].shape[-2:]
    groups = sources // QUART
    tail = (pair, 2, frames, slots)
    depth = QUART * 2 * frames
    firsts, seconds, first_specs, second_specs = [], [], [], []
    for kind, *arrays in datas:
        firsts.append(arrays[0])
        if kind == "whole":
            seconds.append(arrays[0])
            for part, specs in ((0, first_specs), (1, second_specs)):
                specs.append(
                    pl.BlockSpec((sources, 1, *tail), lambda k, _, part=part: (0, part, k, 0, 0, 0))
                )
        else:
            seconds.append(arrays[1])
            member = arrays[2]
            first_specs.append(pl.BlockSpec((sources, *tail), lambda k, _: (0, k, 0, 0, 0)))
            second_specs.append(
                pl.BlockSpec(
                    (groups, 1, *tail), lambda k, _, member=member: (0, member, k, 0, 0, 0)
                )
            )
    operands = [quarter, order, *firsts, *seconds]
    in_specs = [pl.BlockSpec((1, inputs), lambda k, _: (0, 0)), *first_specs, *second_specs]
    aliases = {}
    scale = 1.0 / (QUART * frames)
    if earlier is not None:
        aliases = {len(operands): 0}
        operands.append(earlier)
        in_specs.append(pl.BlockSpec(memory_space=pl.ANY))
    kinds = tuple(data[0] for data in datas)
    return pl.pallas_call(
        functools.partial(back_kernel, kinds, groups, pair, scale),
        grid_spec=pltpu.PrefetchScalarGridSpec(
            num_scalar_prefetch=1,
            grid=(steps,),
            in_specs=in_specs,
            out_specs=pl.BlockSpec((pair, inputs, inputs), lambda k, _: (k + each * steps, 0, 0)),
            scratch_shapes=[
                pltpu.VMEM((inputs, inputs), jnp.bfloat16),
                pltpu.VMEM((inputs, pair * depth), jnp.bfloat16),
                pltpu.VMEM((inputs, pair * depth), jnp.bfloat16),
            ],
        ),
        out_shape=jax.ShapeDtypeStruct((chan_dev, inputs, inputs), jnp.bfloat16),
        input_output_aliases=aliases,
        cost_estimate=pl.CostEstimate(
            flops=held * inputs * inputs * 1024,
            bytes_accessed=2 * held * inputs * inputs,
            transcendentals=0,
        ),
        name="back",
    )(*operands)


def hops(values, plane, upward):
    moved = []
    for target, value in values:
        if upward:
            senders, step = range(target), plane
        else:
            senders, step = range(target + 1, QUART), -plane
        places = [quarter * plane + i for quarter in senders for i in range(plane)]
        moved.append(lax.ppermute(value, "chan", [(place, place + step) for place in places]))
    return moved


def after(value, earlier):
    return lax.optimization_barrier((value, earlier))[0]


def exchange(value):
    return lax.all_to_all(value, "chan", split_axis=0, concat_axis=0, tiled=True)


def on_device(samples, fir, chan_assign, input_order):
    own_frames = samples[0]
    _, slots_dev, frame_len = own_frames.shape
    chan_count = lax.axis_size("chan")
    plane = chan_count // QUART
    chan_dev = chan_assign.shape[0] // chan_count
    sets = 2 if chan_dev % 2 == 0 else 1
    held = chan_dev // sets
    blocks = 2 if slots_dev % (2 * LANES) == 0 else 1
    chans = chan_assign.reshape(chan_count, sets, held).transpose(1, 0, 2).reshape(-1)
    fine, coarse = split_table(chans, frame_len)
    order = input_order[None, :]
    quarter = (lax.axis_index("chan") // plane).astype(jnp.int32)[None]
    planes = [[q * plane + i for i in range(plane)] for q in range(QUART)]

    ready = [[None] * blocks for _ in range(sets)]
    source, token, pending = own_frames, None, []
    for block in range(blocks):
        if block == 0:
            groups = [((0,), True)] + [((each,), False) for each in range(1, sets)]
        else:
            groups = [(tuple(range(sets)), False)]
        parts = front(source, fir, fine, coarse, block, blocks, groups, chan_count)
        source = after(own_frames, parts[0])
        for members, whole in groups:
            if whole:
                token = exchange(parts[0])
                ready[members[0]][block] = ("whole", token)
                parts = parts[1:]
                continue
            owns, lates, parts = parts[:QUART], parts[QUART : 2 * QUART], parts[2 * QUART :]
            risen = hops(list(enumerate(lates))[1:], plane, True)
            fallen = hops(list(enumerate(owns))[:-1], plane, False)
            pending.append((block, members, owns, lates, risen, fallen))
    for block, members, owns, lates, risen, fallen in pending:
        *met, side = meet(quarter, [after(owns[0], token), *owns[1:]], lates, risen, fallen)
        swapped = []
        for index in range(len(members)):
            block_met = met[index].reshape(chan_count, *met[index].shape[2:])
            if index:
                block_met = after(block_met, side)
            token = exchange(block_met)
            swapped.append(token)
            if index == 0:
                side = lax.all_to_all(
                    after(side, token),
                    "chan",
                    split_axis=0,
                    concat_axis=0,
                    axis_index_groups=planes,
                    tiled=True,
                )
        for index, each in enumerate(members):
            ready[each][block] = ("met", swapped[index], side, index)
    vis = None
    for each in range(sets):
        vis = back(quarter, order, ready[each], each, sets, chan_dev, vis)
    return vis


def solution(mesh):
    in_specs = (P(("grp", "chan"), None, None, None), P(), P(), P())
    out_specs = P(("grp", "chan"), None, None)


    return jax.shard_map(
        on_device, mesh=mesh, in_specs=in_specs, out_specs=out_specs, check_vma=False
    )
```

```python
import functools
import math

import jax
import jax.numpy as jnp
from jax import lax
from jax.experimental import pallas as pl
from jax.experimental.pallas import tpu as pltpu
from jax.sharding import PartitionSpec as P


QUART = 4
LANES = 128


def split_table(chans, frame_len):
    norm_scale = 1.0 / math.sqrt(frame_len)

    def angles(samples):
        phase_index = chans[:, None] * samples[None, :] % frame_len
        return phase_index.astype(jnp.float32) * (2.0 * math.pi / frame_len)

    fine = angles(jnp.arange(LANES, dtype=jnp.int32))
    coarse = angles(jnp.arange(0, frame_len, LANES, dtype=jnp.int32)).T
    return jnp.cos(fine) * norm_scale, jnp.sin(fine) * norm_scale, jnp.cos(coarse), jnp.sin(coarse)


def tap_leaves(taps):
    if len(taps) <= 4:
        return [taps]
    low, high = taps[: len(taps) // 2], taps[len(taps) // 2 :]
    middle = [one + other for one, other in zip(low, high)]
    return tap_leaves(low) + tap_leaves(high) + tap_leaves(middle)


def direct(values, taps):
    outs = []
    for out in range(len(values) + len(taps) - 1):
        total = None
        for source in range(max(0, out - len(taps) + 1), min(len(values), out + 1)):
            term = values[source] * taps[out - source]
            total = term if total is None else total + term
        outs.append(total)
    return outs


def product(values, leaves):
    count = len(values)
    if count <= 4:
        return direct(values, next(leaves))
    half = count // 2
    low = product(values[:half], leaves)
    high = product(values[half:], leaves)
    middle = product([one + other for one, other in zip(values[:half], values[half:])], leaves)
    middle = [whole - (one + other) for whole, one, other in zip(middle, low, high)]
    outs = low[:half]
    outs += [low[half + i] + middle[i] for i in range(half - 1)]
    outs += [middle[half - 1]]
    outs += [middle[half + i] + high[i] for i in range(half - 1)]
    return outs + high[half - 1 :]


def front_kernel(groups, x_ref, fir_ref, cos_ref, sin_ref, cos_turn, sin_turn, *rest):
    outs, (filt, table, coeffs, spread) = rest[:-4], rest[-4:]
    sets = sum(len(members) for members, _ in groups)
    frames, slots, lanes = x_ref.shape
    taps = fir_ref.shape[0]
    step = pl.program_id(0)
    columns = pl.ds(pl.multiple_of(step * lanes, lanes), lanes)
    recursive = taps == frames and frames & (frames - 1) == 0

    chans = cos_ref.shape[0]
    turns = [
        jnp.broadcast_to(turn[pl.ds(step, 1), :], (lanes, chans)).T for turn in (cos_turn, sin_turn)
    ]
    real = cos_ref[...] * turns[0] - sin_ref[...] * turns[1]
    imag = -(sin_ref[...] * turns[0] + cos_ref[...] * turns[1])
    table[:chans, columns] = real.astype(jnp.bfloat16)
    table[chans:, columns] = imag.astype(jnp.bfloat16)

    leaves = [fir_ref[tap : tap + 1, :] for tap in range(taps)]
    leaves = tap_leaves(leaves) if recursive else [leaves]
    sizes = [len(leaf) for leaf in leaves]
    for index, row in enumerate(sum(leaves, [])):
        coeffs[index : index + 1, :] = row

    def filter_rows(block, carry):
        rows = pl.ds(pl.multiple_of(block * 16, 16), 16)
        own = [x_ref[f, rows, :].astype(jnp.float32) for f in range(frames)]
        done = []
        for half in range(2):
            values = [one[half * 8 : half * 8 + 8] for one in own]
            starts = [sum(sizes[:i]) for i in range(len(sizes))]
            lists = [
                [coeffs[start + i : start + i + 1, :] for i in range(size)]
                for start, size in zip(starts, sizes)
            ]
            results = product(values, iter(lists)) if recursive else direct(values, lists[0])
            done.append(results)
        for out in range(2 * frames):
            if out < len(done[0]):
                total = jnp.concatenate([done[0][out], done[1][out]], axis=0)
            else:
                total = jnp.zeros((16, lanes), jnp.float32)
            filt[out, rows, columns] = total.astype(jnp.bfloat16)
        return carry

    lax.fori_loop(0, slots // 16, filter_rows, 0)

    def deliver(part, which, values):
        first = 0
        for members, whole in groups:
            refs = outs[first : first + (1 if whole else 2 * QUART)]
            first += len(refs)
            per_dest = refs[0].shape[2]
            shaped = values.reshape(-1, sets, per_dest, frames, slots)
            for index, each in enumerate(members):
                mine = shaped[:, each].astype(jnp.bfloat16)
                if whole:
                    refs[0][:, part, :, which] = mine
                    continue
                plane = mine.shape[0] // QUART
                for target in range(QUART):
                    out = refs[part * QUART + target]
                    out[index, :, :, which] = mine[target * plane : (target + 1) * plane]

    @pl.when(step == pl.num_programs(0) - 1)
    def _():
        contract = (((1,), (1,)), ((), ()))
        for part in range(2):
            if slots % LANES == 0:
                result = lax.dot_general(
                    table[...],
                    filt[part * frames : (part + 1) * frames].reshape(frames * slots, -1),
                    contract,
                    preferred_element_type=jnp.float32,
                )
                result = result.reshape(-1, frames, slots)
                for which in range(2):
                    deliver(part, which, result[which * chans : (which + 1) * chans])
            else:

                def transform(frame, carry):
                    result = lax.dot_general(
                        table[...],
                        filt[part * frames + frame],
                        contract,
                        preferred_element_type=jnp.float32,
                    )
                    spread[pl.ds(frame, 2 * chans, stride=frames), :] = result
                    return carry

                lax.fori_loop(0, frames, transform, 0)
                for which in range(2):
                    values = spread[which * chans * frames : (which + 1) * chans * frames, :]
                    deliver(part, which, values.reshape(chans, frames, slots))


def front(x, fir, angles, block, blocks, groups, dests):
    frames, slots_dev, frame_len = x.shape
    slots = slots_dev // blocks
    taps = fir.shape[0]
    chans = angles[0].shape[0]
    sets = sum(len(members) for members, _ in groups)
    tail = (chans // sets // dests, 2, frames, slots)
    shapes = []
    for members, whole in groups:
        if whole:
            shapes += [(dests, 2, tail[0], *tail[1:])]
        else:
            shapes += [(len(members), dests // QUART, *tail)] * (2 * QUART)
    spread = (8, LANES) if slots % LANES == 0 else (2 * chans * frames, slots)
    return pl.pallas_call(
        functools.partial(front_kernel, groups),
        grid=(frame_len // LANES,),
        in_specs=[
            pl.BlockSpec((frames, slots, LANES), lambda j: (0, block, j)),
            pl.BlockSpec((taps, LANES), lambda j: (0, j)),
        ]
        + [
            pl.BlockSpec(angle.shape, lambda j: (0, 0), pipeline_mode=pl.Buffered(1))
            for angle in angles
        ],
        out_specs=[
            pl.BlockSpec(shape, lambda j: (0, 0, 0, 0, 0, 0), pipeline_mode=pl.Buffered(1))
            for shape in shapes
        ],
        out_shape=[jax.ShapeDtypeStruct(shape, jnp.bfloat16) for shape in shapes],
        scratch_shapes=[
            pltpu.VMEM((2 * frames, slots, frame_len), jnp.bfloat16),
            pltpu.VMEM((2 * chans, frame_len), jnp.bfloat16),
            pltpu.VMEM((4 * taps, LANES), jnp.float32),
            pltpu.VMEM(spread, jnp.float32),
        ],
        cost_estimate=pl.CostEstimate(
            flops=8 * frames * slots * frame_len * chans,
            bytes_accessed=2 * frames * slots * frame_len + 8 * chans * frames * slots,
            transcendentals=0,
        ),
        name="front",
    )(x, fir, *angles)


def meet_kernel(sets, where_ref, *refs):
    owns, lates = refs[:QUART], refs[QUART : 2 * QUART]
    risen, fallen = refs[2 * QUART : 3 * QUART - 1], refs[3 * QUART - 1 : 4 * QUART - 2]
    outs, sides, hold = refs[4 * QUART - 2 :][:sets], refs[4 * QUART - 2 :][sets:-1], refs[-1]
    here = where_ref[0]
    offset = pl.program_id(0) - where_ref[1]
    offset = jnp.where(offset < 0, offset + len(sides), offset)

    def add(one, other):
        return (one.astype(jnp.float32) + other.astype(jnp.float32)).astype(jnp.bfloat16)

    for target in range(QUART):

        @pl.when(here <= target)
        def _():
            for each in range(sets):
                own = owns[target][each, 0]
                outs[each][target, 0] = add(own, risen[target - 1][each, 0]) if target else own

        if target == QUART - 1:
            continue

        @pl.when(here > target)
        def _():
            for each in range(sets):
                outs[each][target, 0] = add(fallen[target][each, 0], lates[target][each, 0])

        @pl.when(here == target)
        def _():
            for each in range(sets):
                hold[each] = add(fallen[target][each, 0], lates[target][each, 0])

    @pl.when(here == QUART - 1)
    def _():
        hold[...] = jnp.zeros_like(hold)

    for distance, side in enumerate(sides):

        @pl.when(offset == distance)
        def _():
            side[...] = hold[...]


def meet(where, owns, lates, risen, fallen):
    sets, plane, *tail = owns[0].shape
    block = pl.BlockSpec((sets, 1, *tail), lambda g, _: (0, g, 0, 0, 0, 0))
    out = pl.BlockSpec((QUART, 1, *tail), lambda g, _: (0, g, 0, 0, 0, 0))
    side = pl.BlockSpec((sets, *tail), lambda g, _: (0, 0, 0, 0, 0))
    shapes = [(QUART, plane, *tail)] * sets + [(sets, *tail)] * plane
    operands = [*owns, *lates, *risen, *fallen]
    return pl.pallas_call(
        functools.partial(meet_kernel, sets),
        grid_spec=pltpu.PrefetchScalarGridSpec(
            num_scalar_prefetch=1,
            grid=(plane,),
            in_specs=[block] * len(operands),
            out_specs=[out] * sets + [side] * plane,
            scratch_shapes=[pltpu.VMEM((sets, *tail), jnp.bfloat16)],
        ),
        out_shape=[jax.ShapeDtypeStruct(shape, jnp.bfloat16) for shape in shapes],
        cost_estimate=pl.CostEstimate(
            flops=sets * owns[0].size * 5, bytes_accessed=owns[0].size * 40, transcendentals=0
        ),
        name="meet",
    )(where, *operands)


def back_kernel(kinds, groups, pair, scale, where_ref, order_ref, *refs):
    firsts, seconds, used = refs[: len(kinds)], [], len(kinds)
    for kind in kinds:
        count = 1 if kind == "whole" else groups
        seconds.append(refs[used : used + count])
        used += count
    out_ref, pick, ordered, turned = refs[-4:]
    inputs = out_ref.shape[-1]
    tile = min(256, inputs)
    here = where_ref[0]

    @pl.when(pl.program_id(0) == 0)
    def _():
        for first in range(0, inputs, tile):
            wanted = first + lax.broadcasted_iota(jnp.int32, (tile, inputs), 0)
            hit = jnp.where(order_ref[...] == wanted, 1.0, 0.0)
            pick[first : first + tile, :] = hit.astype(jnp.bfloat16)

    def rows_of(kind, first, second, distance, group, place, chan, part):
        if kind == "whole":
            if place == 0:
                return first[group, 0, chan, part]
            quarter = jnp.where(place <= here, place, place + 1)
            if place == QUART - 1:
                quarter = jnp.minimum(here + 1, QUART - 1)
            own = first[quarter * groups + group, 0, chan, part].astype(jnp.float32)
            before = second[0][(quarter - 1) * groups + group, 0, chan, part].astype(jnp.float32)
            return (own + before).astype(jnp.bfloat16)
        value = first[place * groups + group, chan, part]
        if place == QUART - 1:
            value = jnp.where(here < QUART - 1, second[distance][0, chan, part], value)
        return value

    pieces = []
    for distance in range(groups):
        group = where_ref[1] - distance
        group = jnp.where(group < 0, group + groups, group)
        for kind, first, second in zip(kinds, firsts, seconds):
            rows = []
            for chan in range(pair):
                for part in range(2):
                    for place in range(QUART):
                        row = rows_of(kind, first, second, distance, group, place, chan, part)
                        rows.append(row)
            pieces.append(jnp.concatenate(rows, axis=0))
    stacked = jnp.concatenate(pieces, axis=1)
    depth = stacked.shape[0] // pair
    contract = (((1,), (1,)), ((), ()))
    lane = lax.broadcasted_iota(jnp.int32, (tile, depth), 1)
    sign = jnp.where(lane < depth // 2, 1.0, -1.0)
    for first in range(0, inputs, tile):
        part = pl.ds(first, tile)
        result = lax.dot_general(
            pick[part, :], stacked, contract, preferred_element_type=jnp.float32
        )
        ordered[part, :] = result.astype(jnp.bfloat16)
        for chan in range(pair):
            lanes = slice(chan * depth, (chan + 1) * depth)
            swapped = pltpu.roll(result[:, lanes], depth // 2, 1) * sign
            turned[part, lanes] = swapped.astype(jnp.bfloat16)
    for chan in range(pair):
        lanes = slice(chan * depth, (chan + 1) * depth)
        for first in range(0, inputs, tile):
            left = ordered[first : first + tile, lanes]
            for other in range(0, inputs, tile):
                place = pl.ds(other, tile)
                if other >= first:
                    upper = lax.dot_general(
                        left, ordered[place, lanes], contract, preferred_element_type=jnp.float32
                    )
                if other <= first:
                    lower = lax.dot_general(
                        left, turned[place, lanes], contract, preferred_element_type=jnp.float32
                    )
                if other > first:
                    result = upper
                elif other < first:
                    result = lower
                else:
                    row = lax.broadcasted_iota(jnp.int32, (tile, tile), 0)
                    column = lax.broadcasted_iota(jnp.int32, (tile, tile), 1)
                    result = jnp.where(row <= column, upper, lower)
                out_ref[chan, first : first + tile, place] = (result * scale).astype(jnp.bfloat16)


def back(where, order, datas, each, sets, chan_dev, earlier):
    inputs = order.shape[1]
    held = chan_dev // sets
    pair = 2 if held % 2 == 0 else 1
    steps = held // pair
    sources, (frames, slots) = datas[0][1].shape[0], datas[0][1].shape[-2:]
    groups = sources // QUART
    tail = (pair, 2, frames, slots)
    depth = QUART * 2 * frames
    firsts, seconds, first_specs, second_specs = [], [], [], []
    for kind, *arrays in datas:
        firsts.append(arrays[0])
        if kind == "whole":
            seconds.append(arrays[0])
            for part, specs in ((0, first_specs), (1, second_specs)):
                specs.append(
                    pl.BlockSpec((sources, 1, *tail), lambda k, _, part=part: (0, part, k, 0, 0, 0))
                )
        else:
            seconds += arrays[1]
            member = arrays[2]
            first_specs.append(pl.BlockSpec((sources, *tail), lambda k, _: (0, k, 0, 0, 0)))
            second_specs += [
                pl.BlockSpec((1, *tail), lambda k, _, member=member: (member, k, 0, 0, 0))
            ] * groups
    operands = [where, order, *firsts, *seconds]
    in_specs = [pl.BlockSpec((1, inputs), lambda k, _: (0, 0)), *first_specs, *second_specs]
    aliases = {}
    scale = 1.0 / (QUART * frames)
    if earlier is not None:
        aliases = {len(operands): 0}
        operands.append(earlier)
        in_specs.append(pl.BlockSpec(memory_space=pl.ANY))
    kinds = tuple(data[0] for data in datas)
    return pl.pallas_call(
        functools.partial(back_kernel, kinds, groups, pair, scale),
        grid_spec=pltpu.PrefetchScalarGridSpec(
            num_scalar_prefetch=1,
            grid=(steps,),
            in_specs=in_specs,
            out_specs=pl.BlockSpec((pair, inputs, inputs), lambda k, _: (k + each * steps, 0, 0)),
            scratch_shapes=[
                pltpu.VMEM((inputs, inputs), jnp.bfloat16),
                pltpu.VMEM((inputs, pair * depth), jnp.bfloat16),
                pltpu.VMEM((inputs, pair * depth), jnp.bfloat16),
            ],
        ),
        out_shape=jax.ShapeDtypeStruct((chan_dev, inputs, inputs), jnp.bfloat16),
        input_output_aliases=aliases,
        cost_estimate=pl.CostEstimate(
            flops=held * inputs * inputs * 1024,
            bytes_accessed=2 * held * inputs * inputs,
            transcendentals=0,
        ),
        name="back",
    )(*operands)


def hops(values, plane, upward):
    moved = []
    for target, value in values:
        if upward:
            senders, step = range(target), plane
        else:
            senders, step = range(target + 1, QUART), -plane
        places = [quarter * plane + i for quarter in senders for i in range(plane)]
        moved.append(lax.ppermute(value, "chan", [(place, place + step) for place in places]))
    return moved


def after(value, earlier):
    return lax.optimization_barrier((value, earlier))[0]


def mark(value):
    def kernel(value_ref, out_ref):
        out_ref[...] = value_ref[...]

    shape = jax.ShapeDtypeStruct(value.shape, value.dtype)
    return pl.pallas_call(kernel, out_shape=shape, name="mark")(value)


def exchange(value):
    return lax.all_to_all(value, "chan", split_axis=0, concat_axis=0, tiled=True)


def on_device(samples, fir, chan_assign, input_order):
    own_frames = samples[0]
    _, slots_dev, frame_len = own_frames.shape
    chan_count = lax.axis_size("chan")
    plane = chan_count // QUART
    chan_dev = chan_assign.shape[0] // chan_count
    sets = 2 if chan_dev % 2 == 0 else 1
    blocks = 2 if slots_dev % (2 * LANES) == 0 else 1
    angles = split_table(chan_assign, frame_len)
    here = lax.axis_index("chan").astype(jnp.int32)
    where = jnp.stack([here // plane, here % plane])
    order = jnp.concatenate([input_order, input_order]).reshape(2 * plane, -1)[::-1]
    order = lax.dynamic_slice_in_dim(order, plane - 1 - here % plane, plane).reshape(1, -1)

    ready = [[None] * blocks for _ in range(sets)]
    source, token, pending = own_frames, None, []
    for block in range(blocks):
        if block == 0:
            groups = [((0,), True)] + [((each,), False) for each in range(1, sets)]
        else:
            groups = [(tuple(range(sets)), False)]
        parts = front(source, fir, angles, block, blocks, groups, chan_count)
        source = after(own_frames, parts[0])
        for members, whole in groups:
            if whole:
                token = exchange(parts[0])
                ready[members[0]][block] = ("whole", token)
                parts = parts[1:]
                continue
            owns, lates, parts = parts[:QUART], parts[QUART : 2 * QUART], parts[2 * QUART :]
            risen = hops(list(enumerate(lates))[1:], plane, True)
            fallen = hops(list(enumerate(owns))[:-1], plane, False)
            pending.append((block, members, owns, lates, risen, fallen))
    for block, members, owns, lates, risen, fallen in pending:
        owns = [after(owns[0], token), *owns[1:]]
        met = meet(where, owns, lates, risen, fallen)
        met, sides = met[: len(members)], list(met[len(members) :])
        for distance in range(1, plane):
            moves = [
                (q * plane + i, q * plane + (i + distance) % plane)
                for q in range(QUART)
                for i in range(plane)
            ]
            sides[distance] = lax.ppermute(sides[distance], "chan", moves)
        for index, each in enumerate(members):
            block_met = met[index].reshape(chan_count, *met[index].shape[2:])
            if index:
                block_met = after(block_met, token)
            token = exchange(block_met)
            ready[each][block] = ("met", token, sides, index)
    for _ in range(2):
        order = mark(order)
    vis = None
    for each in range(sets):
        vis = back(where, order, ready[each], each, sets, chan_dev, vis)
    return vis


def solution(mesh):
    in_specs = (P(("grp", "chan"), None, None, None), P(), P(), P())
    out_specs = P(("grp", "chan"), None, None)


    return jax.shard_map(
        on_device, mesh=mesh, in_specs=in_specs, out_specs=out_specs, check_vma=False
    )
```
